32 devices in a mesh: gx: 8 (over z, x), gy: 4 (over y, core).
Axes of the slice: x: 2, y: 2, z: 4, core: 2. Of those that a mesh axis runs over, the one named last changes fastest.
Arguments:
- inputs: bfloat16 [64, 64, 256], P('gx', 'gy'), may hold values from -6 to 6
- coarse: bfloat16 [64, 64, 256], P('gx', 'gy'), may hold values from -6 to 6
- cotangent: bfloat16 [64, 64, 256], P('gx', 'gy'), may hold values from -16 to 16
- enc_weight: bfloat16 [3, 3, 3, 32, 32], replicated, may hold values from -0.21875 to 0.21875
- dec_weight: bfloat16 [3, 3, 3, 64, 32], replicated, may hold values from -0.15625 to 0.15625
Outputs:
- inputs_grad: bfloat16 [64, 64, 256], P('gx', 'gy')
- coarse_grad: bfloat16 [64, 64, 256], P('gx', 'gy')
- enc_weight_grad: float32 [3, 3, 3, 32, 32], replicated
- dec_weight_grad: float32 [3, 3, 3, 64, 32], replicated
The draws below stay inside these ranges and needn't reach their ends.
All inputs are finite; a program needn't handle non-finite values.
Results may differ from the reference program's by a relative error of at most 0.0059.
Values may be sent and summed in bfloat16 or wider, within the bound.
A program may use at most 64 MiB of HBM per device.

```python
import math
import jax
import jax.numpy as jnp
from jax import lax

C = 32
NZ = 8
NX = 64
NY = 64


def draw_cotangent(key, part):
    first = jax.random.fold_in(key, 0)
    row_pos = jnp.arange(NX, dtype=jnp.float32) / NX
    col_pos = jnp.arange(NY, dtype=jnp.float32) / NY
    base = jax.random.normal(first, (NX, NY, NZ * C), jnp.float32)
    values = base * (3.0 ** row_pos)[:, None, None] * (3.0 ** col_pos)[None, :, None]
    return jnp.clip(values, -16.0, 16.0).astype(jnp.bfloat16)


def levels(own_key, extent, shards, least, largest):
    def one(dim, parts):
        steps = jax.random.uniform(jax.random.fold_in(jax.random.fold_in(own_key, 6), dim), (parts,), jnp.float32, least / len(shards), largest / len(shards))
        return jnp.repeat(jnp.exp(steps), extent[dim] // parts).reshape((-1,) + (1,) * (len(extent) - dim - 1))

    loudness = one(*shards[0])
    for cut in shards[1:]:
        loudness = loudness * one(*cut)
    return loudness


def bell_draw(own_key, dims, width, bound, cuts=(), held_as=jnp.bfloat16):
    factor_of = levels(own_key, dims, cuts, -0.22, 0.18) if cuts else 1.0
    entries = jax.random.normal(own_key, dims, jnp.float32) * width * factor_of
    return jnp.minimum(jnp.maximum(entries, -bound), bound).astype(held_as)


def setup_inputs(seed: int = 0) -> dict:
    seeds = jax.random.split(jax.random.key(seed), 6)
    return {
        "inputs": bell_draw(seeds[0], (NX, NY, NZ * C), 1.0, 6.0, ((0, 8), (1, 4))),
        "coarse": bell_draw(seeds[1], (NX, NY, NZ * C), 1.0, 6.0, ((0, 8), (1, 4))),
        "cotangent": draw_cotangent(jax.random.fold_in(seeds[5], 71), 0),
        "enc_weight": bell_draw(seeds[3], (3, 3, 3, C, C), (27 * C) ** -0.5, 0.21875),
        "dec_weight": bell_draw(seeds[4], (3, 3, 3, 2 * C, C), (54 * C) ** -0.5, 0.15625),
    }


def periodic_pad(field):
    padded = jnp.pad(field, ((1, 1), (1, 1), (0, 0), (0, 0)), mode='wrap')
    return jnp.pad(padded, ((0, 0), (0, 0), (1, 1), (0, 0)))

def periodic_conv(field, weight):
    padded = periodic_pad(field)
    result = lax.conv_general_dilated(padded[None], weight, (1, 1, 1), 'VALID', dimension_numbers=('NDHWC', 'DHWIO', 'NDHWC'), precision=lax.Precision.HIGHEST)
    return result[0]

def flipped(weight):
    return jnp.swapaxes(weight[::-1, ::-1, ::-1], 3, 4)

def silu_slope(value):
    sig = jax.nn.sigmoid(value)
    return sig * (1.0 + value * (1.0 - sig))

def rounded(value):
    return lax.optimization_barrier(value.astype(jnp.bfloat16)).astype(jnp.float32)

def kernel_grad(field, delta):
    padded = periodic_pad(field)
    terms = []
    for shift_x in range(3):
        for shift_y in range(3):
            for shift_z in range(3):
                piece = padded[shift_x:shift_x + NX, shift_y:shift_y + NY, shift_z:shift_z + NZ]
                terms.append(jnp.tensordot(piece, delta, axes=((0, 1, 2), (0, 1, 2)), precision=lax.Precision.HIGHEST))
    return jnp.stack(terms).reshape(3, 3, 3, field.shape[3], delta.shape[3])

def reference(inputs, coarse, cotangent, enc_weight, dec_weight):
    shape = (NX, NY, NZ, C)
    feats = inputs.astype(jnp.float32).reshape(shape)
    upper = coarse.astype(jnp.float32).reshape(shape)
    grads = cotangent.astype(jnp.float32).reshape(shape)
    enc_w = enc_weight.astype(jnp.float32)
    dec_w = dec_weight.astype(jnp.float32)
    pre_enc = periodic_conv(feats, enc_w)
    skip = rounded(jax.nn.silu(pre_enc))
    joined = jnp.concatenate([upper, skip], axis=3)
    pre_dec = periodic_conv(joined, dec_w)
    dec_delta = rounded(grads * silu_slope(pre_dec))
    cat_grad = periodic_conv(dec_delta, flipped(dec_w))
    coarse_grad = cat_grad[..., :C].astype(jnp.bfloat16)
    skip_grad = cat_grad[..., C:]
    enc_delta = rounded(skip_grad * silu_slope(pre_enc))
    inputs_grad = periodic_conv(enc_delta, flipped(enc_w)).astype(jnp.bfloat16)
    scale = 1.0 / math.sqrt(NX * NY * NZ)
    dec_weight_grad = kernel_grad(joined, dec_delta) * scale
    enc_weight_grad = kernel_grad(feats, enc_delta) * scale
    flat = (NX, NY, NZ * C)
    return (inputs_grad.reshape(flat), coarse_grad.reshape(flat), enc_weight_grad, dec_weight_grad)
```

```python
import functools
import math

import jax
import jax.numpy as jnp
from jax import lax
from jax.experimental import pallas as pl
from jax.experimental.pallas import tpu as pltpu
from jax.sharding import PartitionSpec as P

MESH = pl.DeviceIdType.MESH
F32 = jnp.float32
BF16 = jnp.bfloat16
BASE = 16
DIRECTIONS = [(dx, dy) for dx in (-1, 0, 1) for dy in (-1, 0, 1) if (dx, dy) != (0, 0)]


def sigmoid(value):
    return 1.0 / (1.0 + jnp.exp(-value))


def slope(value):
    sig = sigmoid(value)
    return sig * (1.0 + value * (1.0 - sig))


def kernel(
    nx, ny, scale,
    inputs, coarse, cotangent, enc_w, dec_w,
    inputs_grad, coarse_grad, enc_out, dec_out,
    enc_band, dec_band,
    mid_in, lo_in, hi_in, slo_in, shi_in,
    mid_co, lo_co, hi_co, slo_co, shi_co,
    mid_de, lo_de, hi_de, slo_de, shi_de,
    mid_en, lo_en, hi_en, slo_en, shi_en,
    wide, ext, near_in, near_co, near_sk, near_de, near_en,
    pre, acc_dec, acc_cat,
    g_dec, r1_dec, h_dec, r2_dec, f_dec,
    g_enc, r1_enc, h_enc, r2_enc, f_enc,
    halo_send, halo_recv, y_sems, x_sems,
):
    ix = lax.axis_index("gx")
    jy = lax.axis_index("gy")
    cx, cy, width = inputs.shape
    cells = cx * cy
    channels = enc_w.shape[2]
    planes = width // channels
    groups = 128 // channels

    def peer(dx, dy):
        return (lax.rem(ix + dx + nx, nx), lax.rem(jy + dy + ny, ny))

    partners = {(dx % nx, dy % ny) for dx, dy in DIRECTIONS}
    partners |= {(k, 0) for k in range(1, nx)} | {(0, k) for k in range(1, ny)}
    barrier = pltpu.get_barrier_semaphore()
    for dx, dy in sorted(partners):
        pl.semaphore_signal(barrier, inc=1, device_id=peer(dx, dy), device_id_type=MESH)

    def stage(value, w, slo, shi):
        slo[...] = value[:, 0:w].astype(F32)
        shi[...] = value[:, cy - w : cy].astype(F32)

    def halo(which, w, mid, lo, hi, slo, shi):
        src_x = {-1: (0, w), 0: (0, cx), 1: (cx - w, w)}
        dst_x = {-1: (cx + w, w), 0: (w, cx), 1: (0, w)}
        copies = []
        for d, (dx, dy) in enumerate(DIRECTIONS):
            start, size = src_x[dx]
            if dy == 0:
                source = mid.at[pl.ds(w + start, size)]
            else:
                source = (slo if dy < 0 else shi).at[pl.ds(start, size)]
            target = {0: mid, -1: hi, 1: lo}[dy].at[pl.ds(dst_x[dx][0], size)]
            copies.append(
                pltpu.make_async_remote_copy(
                    src_ref=source,
                    dst_ref=target,
                    send_sem=halo_send.at[which, d],
                    recv_sem=halo_recv.at[which, d],
                    device_id=peer(dx, dy),
                    device_id_type=MESH,
                )
            )
        return copies

    def start(copies):
        for copy in copies:
            copy.start()

    def arrive(copies):
        for copy in copies:
            copy.wait_recv()

    def fill(target, w, mid, lo, hi):
        target[:, BASE : BASE + cy] = mid[...].astype(F32)
        target[:, BASE - w : BASE] = lo[...]
        target[:, BASE + cy : BASE + cy + w] = hi[...]

    def spread(source, near):
        for b in range(3):
            near[b] = source[:, BASE - 1 + b : BASE - 1 + b + cy].astype(BF16)

    own_in = inputs[...]
    own_co = coarse[...]
    mid_in[2 : 2 + cx] = own_in
    mid_co[1 : 1 + cx] = own_co
    stage(own_in, 2, slo_in, shi_in)
    stage(own_co, 1, slo_co, shi_co)
    pl.semaphore_wait(barrier, len(partners))
    halo_in = halo(0, 2, mid_in, lo_in, hi_in, slo_in, shi_in)
    halo_co = halo(1, 1, mid_co, lo_co, hi_co, slo_co, shi_co)
    start(halo_in)
    start(halo_co)

    spread_mat = (
        lax.broadcasted_iota(jnp.int32, (channels, width), 1) % channels
        == lax.broadcasted_iota(jnp.int32, (channels, width), 0)
    ).astype(F32).astype(BF16)
    plane_of = lax.broadcasted_iota(jnp.int32, (channels, width), 1) // channels

    def band_block(taps, p):
        block = jnp.where(plane_of == p - 1, taps[2], 0.0)
        block = jnp.where(plane_of == p, taps[1], block)
        return jnp.where(plane_of == p + 1, taps[0], block).astype(BF16)

    def make_bands(t, carry):
        enc = jnp.dot(enc_w[t], spread_mat, preferred_element_type=F32)
        dec = jnp.dot(dec_w[t], spread_mat, preferred_element_type=F32)
        enc_taps = [enc[c * channels : (c + 1) * channels] for c in range(3)]
        dec_taps = [
            [dec[(2 * c + s) * channels : (2 * c + s + 1) * channels] for c in range(3)]
            for s in range(2)
        ]
        for p in range(planes):
            rows = slice(p * channels, (p + 1) * channels)
            enc_band[t, rows] = band_block(enc_taps, p)
            for s in range(2):
                dec_band[t, s * width + p * channels : s * width + (p + 1) * channels] = band_block(
                    dec_taps[s], p
                )
        return carry

    lax.fori_loop(0, 9, make_bands, 0)

    wide[...] = jnp.zeros_like(wide)
    pre[...] = jnp.zeros_like(pre)
    acc_dec[...] = jnp.zeros_like(acc_dec)
    acc_cat[...] = jnp.zeros_like(acc_cat)
    g_dec[...] = jnp.zeros_like(g_dec)
    g_enc[...] = jnp.zeros_like(g_enc)

    arrive(halo_in)
    fill(wide, 2, mid_in, lo_in, hi_in)
    for b in range(3):
        near_in[b, :, 0:cy] = wide[:, BASE - 1 + b : BASE - 1 + b + cy].astype(BF16)
        tail = jnp.concatenate(
            [
                wide[:, BASE + cy - 1 + b : BASE + cy + 7 + b],
                wide[:, BASE - 9 + b : BASE - 1 + b],
            ],
            axis=1,
        )
        near_in[b, :, cy : cy + 16] = tail.astype(BF16)

    def enc_step(t, carry):
        a, b = t // 3, t % 3
        piece = near_in[b, pl.ds(a, cx + 2)].reshape((cx + 2) * (cy + 16), width)
        pre[...] += jnp.dot(piece, enc_band[t], preferred_element_type=F32)
        return carry

    lax.fori_loop(0, 9, enc_step, 0)

    value = pre[...].reshape(cx + 2, cy + 16, width)
    skip = (value * sigmoid(value)).astype(BF16).astype(F32)
    ext[:, BASE : BASE + cy] = skip[:, 0:cy]
    ext[:, BASE + cy : BASE + cy + 8] = skip[:, cy : cy + 8]
    ext[:, BASE - 8 : BASE] = skip[:, cy + 8 : cy + 16]
    spread(ext, near_sk)

    arrive(halo_co)
    fill(ext, 1, mid_co, lo_co, hi_co)
    spread(ext, near_co)

    def tap(near, t):
        a, b = t // 3, t % 3
        return near[b, pl.ds(a, cx)].reshape(cells, width)

    def tap_back(near, t):
        a, b = t // 3, t % 3
        return near[2 - b, pl.ds(2 - a, cx)].reshape(cells, width)

    def dec_step(t, carry):
        acc_dec[...] += jnp.dot(
            tap(near_co, t), dec_band[t, 0:width], preferred_element_type=F32
        ) + jnp.dot(tap(near_sk, t), dec_band[t, width : 2 * width], preferred_element_type=F32)
        return carry

    lax.fori_loop(0, 9, dec_step, 0)

    dec_own = (cotangent[...].astype(F32).reshape(cells, width) * slope(acc_dec[...])).astype(BF16)
    dec_cells = dec_own.reshape(cx, cy, width)
    mid_de[1 : 1 + cx] = dec_cells
    stage(dec_cells, 1, slo_de, shi_de)
    halo_de = halo(2, 1, mid_de, lo_de, hi_de, slo_de, shi_de)
    start(halo_de)

    group_of = lax.broadcasted_iota(jnp.int32, (channels, 128), 1) // channels
    row_group = lax.broadcasted_iota(jnp.int32, (8, 128), 1) // channels

    def by_group(index, parts):
        out = parts[-1]
        for g in range(len(parts) - 2, -1, -1):
            out = jnp.where(index == g, parts[g], out)
        return out

    def fold(product, c):
        parts = []
        for g in range(groups):
            total = None
            for z in range(g, planes, groups):
                p = z + c - 1
                if 0 <= p < planes:
                    lane = (z // groups) * 128
                    term = product[p * channels : (p + 1) * channels, lane : lane + 128]
                    total = term if total is None else total + term
            parts.append(total)
        both = by_group(group_of, parts)
        step = 64
        while step >= channels:
            both = both + pltpu.roll(both, step, 1)
            step //= 2
        return by_group(row_group, [both[8 * g : 8 * g + 8] for g in range(groups)])

    def contract(piece, delta):
        return lax.dot_general(piece, delta, (((0,), (0,)), ((), ())), preferred_element_type=F32)

    def dec_taps_step(t, carry):
        delta = mid_de[1 : 1 + cx].reshape(cells, width)
        for s, near in enumerate((near_co, near_sk)):
            product = contract(tap(near, t), delta)
            for c in range(3):
                g_dec[(t * 3 + c) * 2 + s] = fold(product, c)
        return carry

    lax.fori_loop(0, 9, dec_taps_step, 0)

    class Reduce:
        def __init__(self, which, g, r1, h, r2, f):
            self.g, self.r1, self.h, self.r2, self.f = g, r1, h, r2, f
            self.p1 = h.shape[0]
            self.p2 = r2.shape[1]
            mine = jy * self.p1 + ix * self.p2
            self.mine = mine
            self.y_scatter = []
            self.y_gather = []
            for k in range(1, ny):
                there = lax.rem(jy + k, ny)
                for phase, src, dst in (
                    (0, g.at[pl.ds(there * self.p1, self.p1)], r1.at[k - 1]),
                    (1, f.at[pl.ds(jy * self.p1, self.p1)], f.at[pl.ds(jy * self.p1, self.p1)]),
                ):
                    (self.y_scatter, self.y_gather)[phase].append(
                        pltpu.make_async_remote_copy(
                            src_ref=src,
                            dst_ref=dst,
                            send_sem=y_sems.at[which, phase, 0, k - 1],
                            recv_sem=y_sems.at[which, phase, 1, k - 1],
                            device_id=(ix, there),
                            device_id_type=MESH,
                        )
                    )
            self.x_scatter = []
            self.x_gather = []
            for k in range(1, nx):
                there = lax.rem(ix + k, nx)
                for phase, src, dst in (
                    (0, h.at[pl.ds(there * self.p2, self.p2)], r2.at[k - 1]),
                    (1, f.at[pl.ds(mine, self.p2)], f.at[pl.ds(mine, self.p2)]),
                ):
                    (self.x_scatter, self.x_gather)[phase].append(
                        pltpu.make_async_remote_copy(
                            src_ref=src,
                            dst_ref=dst,
                            send_sem=x_sems.at[which, phase, 0, k - 1],
                            recv_sem=x_sems.at[which, phase, 1, k - 1],
                            device_id=(there, jy),
                            device_id_type=MESH,
                        )
                    )

        def step1(self):
            start(self.y_scatter)

        def step2(self):
            arrive(self.y_scatter)
            total = self.g[pl.ds(jy * self.p1, self.p1)]
            for k in range(ny - 1):
                total = total + self.r1[k]
            self.h[...] = total
            start(self.x_scatter)

        def step3(self):
            arrive(self.x_scatter)
            total = self.h[pl.ds(ix * self.p2, self.p2)]
            for k in range(nx - 1):
                total = total + self.r2[k]
            self.f[pl.ds(self.mine, self.p2)] = total * scale
            start(self.x_gather)

        def step4(self):
            arrive(self.x_gather)
            start(self.y_gather)

        def step5(self):
            arrive(self.y_gather)

        def drain(self):
            for copy in self.y_scatter + self.x_scatter + self.x_gather + self.y_gather:
                copy.wait_send()

    dec_sum = Reduce(0, g_dec, r1_dec, h_dec, r2_dec, f_dec)
    enc_sum = Reduce(1, g_enc, r1_enc, h_enc, r2_enc, f_enc)
    dec_sum.step1()

    arrive(halo_de)
    fill(ext, 1, mid_de, lo_de, hi_de)
    spread(ext, near_de)

    def cat_step(t, carry):
        acc_cat[...] += lax.dot_general(
            tap_back(near_de, t), dec_band[t], (((1,), (1,)), ((), ())), preferred_element_type=F32
        )
        return carry

    lax.fori_loop(0, 9, cat_step, 0)
    coarse_grad[...] = acc_cat[:, 0:width].astype(BF16).reshape(cx, cy, width)
    pre_own = pre[...].reshape(cx + 2, cy + 16, width)[1 : 1 + cx, 0:cy].reshape(cells, width)
    enc_own = (acc_cat[:, width : 2 * width] * slope(pre_own)).astype(BF16)
    enc_cells = enc_own.reshape(cx, cy, width)
    mid_en[1 : 1 + cx] = enc_cells
    stage(enc_cells, 1, slo_en, shi_en)
    halo_en = halo(3, 1, mid_en, lo_en, hi_en, slo_en, shi_en)
    start(halo_en)
    dec_sum.step2()

    def enc_taps_step(t, carry):
        a, b = t // 3, t % 3
        delta = mid_en[1 : 1 + cx].reshape(cells, width)
        piece = near_in[b, pl.ds(a + 1, cx), 0:cy].reshape(cells, width)
        product = contract(piece, delta)
        for c in range(3):
            g_enc[t * 3 + c] = fold(product, c)
        return carry

    lax.fori_loop(0, 9, enc_taps_step, 0)
    enc_sum.step1()
    dec_sum.step3()

    arrive(halo_en)
    fill(ext, 1, mid_en, lo_en, hi_en)
    spread(ext, near_en)
    enc_sum.step2()
    acc_dec[...] = jnp.zeros_like(acc_dec)

    def back_step(t, carry):
        acc_dec[...] += lax.dot_general(
            tap_back(near_en, t), enc_band[t], (((1,), (1,)), ((), ())), preferred_element_type=F32
        )
        return carry

    lax.fori_loop(0, 9, back_step, 0)
    inputs_grad[...] = acc_dec[...].astype(BF16).reshape(cx, cy, width)

    enc_sum.step3()
    dec_sum.step4()
    enc_sum.step4()
    dec_sum.step5()

    def unpack_dec(t, carry):
        tile = f_dec[t]
        for g in range(groups):
            dec_out[t, g] = tile[:, g * channels : (g + 1) * channels]
        return carry

    lax.fori_loop(0, dec_out.shape[0], unpack_dec, 0)
    enc_sum.step5()

    def unpack_enc(t, carry):
        tile = f_enc[t]
        for g in range(groups):
            enc_out[t, g] = tile[:, g * channels : (g + 1) * channels]
        return carry

    lax.fori_loop(0, enc_out.shape[0], unpack_enc, 0)

    for copies in (halo_in, halo_co, halo_de, halo_en):
        for copy in copies:
            copy.wait_send()
    dec_sum.drain()
    enc_sum.drain()


def body(nx, ny, inputs, coarse, cotangent, enc_weight, dec_weight):
    cx, cy, width = inputs.shape
    channels = enc_weight.shape[3]
    planes = width // channels
    groups = 128 // channels
    rows = channels // groups
    cells = cx * cy
    scale = 1.0 / math.sqrt(cx * nx * cy * ny * planes)

    def halo_buffers(w):
        return [
            pltpu.VMEM((cx + 2 * w, cy, width), BF16),
            pltpu.VMEM((cx + 2 * w, w, width), F32),
            pltpu.VMEM((cx + 2 * w, w, width), F32),
            pltpu.VMEM((cx, w, width), F32),
            pltpu.VMEM((cx, w, width), F32),
        ]

    def sum_buffers(tiles):
        p2 = -(-tiles // (nx * ny))
        p1 = p2 * nx
        return [
            pltpu.VMEM((p1 * ny, 8, 128), F32),
            pltpu.VMEM((ny - 1, p1, 8, 128), F32),
            pltpu.VMEM((p1, 8, 128), F32),
            pltpu.VMEM((nx - 1, p2, 8, 128), F32),
            pltpu.VMEM((p1 * ny, 8, 128), F32),
        ]

    near = pltpu.VMEM((3, cx + 2, cy, width), BF16)
    vmem = pl.BlockSpec(memory_space=pltpu.VMEM)
    inputs_grad, coarse_grad, enc_total, dec_total = pl.pallas_call(
        functools.partial(kernel, nx, ny, scale),
        out_shape=(
            jax.ShapeDtypeStruct((cx, cy, width), BF16),
            jax.ShapeDtypeStruct((cx, cy, width), BF16),
            jax.ShapeDtypeStruct((27, groups, rows, channels), F32),
            jax.ShapeDtypeStruct((54, groups, rows, channels), F32),
        ),
        in_specs=[vmem] * 5,
        out_specs=(vmem,) * 4,
        scratch_shapes=[
            pltpu.VMEM((9, width, width), BF16),
            pltpu.VMEM((9, 2 * width, width), BF16),
            *halo_buffers(2),
            *halo_buffers(1),
            *halo_buffers(1),
            *halo_buffers(1),
            pltpu.VMEM((cx + 4, cy + 32, width), F32),
            pltpu.VMEM((cx + 2, cy + 32, width), F32),
            pltpu.VMEM((3, cx + 4, cy + 16, width), BF16),
            near,
            near,
            near,
            near,
            pltpu.VMEM(((cx + 2) * (cy + 16), width), F32),
            pltpu.VMEM((cells, width), F32),
            pltpu.VMEM((cells, 2 * width), F32),
            *sum_buffers(54),
            *sum_buffers(27),
            pltpu.SemaphoreType.DMA((4, 8)),
            pltpu.SemaphoreType.DMA((4, 8)),
            pltpu.SemaphoreType.DMA((2, 2, 2, ny - 1)),
            pltpu.SemaphoreType.DMA((2, 2, 2, nx - 1)),
        ],
        compiler_params=pltpu.CompilerParams(
            collective_id=0, has_side_effects=True, vmem_limit_bytes=48 << 20
        ),
    )(
        inputs,
        coarse,
        cotangent,
        enc_weight.reshape(9, 3 * channels, channels),
        dec_weight.reshape(9, 6 * channels, channels),
    )
    return (
        inputs_grad,
        coarse_grad,
        enc_total.reshape(3, 3, 3, channels, channels),
        dec_total.reshape(3, 3, 3, 2 * channels, channels),
    )


def solution(mesh):
    in_specs = (P("gx", "gy", None), P("gx", "gy", None), P("gx", "gy", None), P(), P())
    out_specs = (P("gx", "gy", None), P("gx", "gy", None), P(), P())
    return jax.shard_map(
        functools.partial(body, mesh.shape["gx"], mesh.shape["gy"]),
        mesh=mesh,
        in_specs=in_specs,
        out_specs=out_specs,
        check_vma=False,
    )
```

```python
import functools
import math

import jax
import jax.numpy as jnp
from jax import lax
from jax.experimental import pallas as pl
from jax.experimental.pallas import tpu as pltpu
from jax.sharding import PartitionSpec as P

MESH = pl.DeviceIdType.MESH
F32 = jnp.float32
BF16 = jnp.bfloat16
BASE = 16
DIRECTIONS = [(dx, dy) for dx in (-1, 0, 1) for dy in (-1, 0, 1) if (dx, dy) != (0, 0)]


def sigmoid(value):
    return 1.0 / (1.0 + jnp.exp(-value))


def slope(value):
    sig = sigmoid(value)
    return sig * (1.0 + value * (1.0 - sig))


def kernel(
    nx, ny, scale,
    inputs, coarse, cotangent, enc_w, dec_w,
    inputs_grad, coarse_grad, enc_out, dec_out,
    enc_band, dec_band,
    mid_in, lo_in, hi_in, slo_in, shi_in,
    mid_co, lo_co, hi_co, slo_co, shi_co,
    mid_de, lo_de, hi_de, slo_de, shi_de,
    mid_en, lo_en, hi_en, slo_en, shi_en,
    wide, ext, near_in, near_co, near_sk, near_de, near_en,
    pre, acc_dec, acc_cat,
    g_dec, r1_dec, h_dec, r2_dec, f_dec,
    g_enc, r1_enc, h_enc, r2_enc, f_enc,
    halo_send, halo_recv, y_sems, x_sems,
):
    ix = lax.axis_index("gx")
    jy = lax.axis_index("gy")
    cx, cy, width = inputs.shape
    cells = cx * cy
    channels = enc_w.shape[2]
    planes = width // channels
    groups = 128 // channels

    def peer(dx, dy):
        return (lax.rem(ix + dx + nx, nx), lax.rem(jy + dy + ny, ny))

    partners = {(dx % nx, dy % ny) for dx, dy in DIRECTIONS}
    partners |= {(k, 0) for k in range(1, nx)} | {(0, k) for k in range(1, ny)}
    barrier = pltpu.get_barrier_semaphore()
    for dx, dy in sorted(partners):
        pl.semaphore_signal(barrier, inc=1, device_id=peer(dx, dy), device_id_type=MESH)

    def stage(value, w, slo, shi):
        slo[...] = value[:, 0:w].astype(F32)
        shi[...] = value[:, cy - w : cy].astype(F32)

    def halo(which, w, mid, lo, hi, slo, shi):
        src_x = {-1: (0, w), 0: (0, cx), 1: (cx - w, w)}
        dst_x = {-1: (cx + w, w), 0: (w, cx), 1: (0, w)}
        copies = []
        for d, (dx, dy) in enumerate(DIRECTIONS):
            start, size = src_x[dx]
            if dy == 0:
                source = mid.at[pl.ds(w + start, size)]
            else:
                source = (slo if dy < 0 else shi).at[pl.ds(start, size)]
            target = {0: mid, -1: hi, 1: lo}[dy].at[pl.ds(dst_x[dx][0], size)]
            copies.append(
                pltpu.make_async_remote_copy(
                    src_ref=source,
                    dst_ref=target,
                    send_sem=halo_send.at[which, d],
                    recv_sem=halo_recv.at[which, d],
                    device_id=peer(dx, dy),
                    device_id_type=MESH,
                )
            )
        return copies

    def start(copies):
        for copy in copies:
            copy.start()

    def arrive(copies):
        for copy in copies:
            copy.wait_recv()

    def fill(target, w, mid, lo, hi):
        target[:, BASE : BASE + cy] = mid[...].astype(F32)
        target[:, BASE - w : BASE] = lo[...]
        target[:, BASE + cy : BASE + cy + w] = hi[...]

    def spread(source, near):
        for b in range(3):
            near[b] = source[:, BASE - 1 + b : BASE - 1 + b + cy].astype(BF16)

    own_in = inputs[...]
    own_co = coarse[...]
    mid_in[2 : 2 + cx] = own_in
    mid_co[1 : 1 + cx] = own_co
    stage(own_in, 2, slo_in, shi_in)
    stage(own_co, 1, slo_co, shi_co)
    pl.semaphore_wait(barrier, len(partners))
    halo_in = halo(0, 2, mid_in, lo_in, hi_in, slo_in, shi_in)
    halo_co = halo(1, 1, mid_co, lo_co, hi_co, slo_co, shi_co)
    start(halo_in)
    start(halo_co)

    spread_mat = (
        lax.broadcasted_iota(jnp.int32, (channels, width), 1) % channels
        == lax.broadcasted_iota(jnp.int32, (channels, width), 0)
    ).astype(F32).astype(BF16)
    plane_of = lax.broadcasted_iota(jnp.int32, (channels, width), 1) // channels

    def band_block(taps, p):
        block = jnp.where(plane_of == p - 1, taps[2], 0.0)
        block = jnp.where(plane_of == p, taps[1], block)
        return jnp.where(plane_of == p + 1, taps[0], block).astype(BF16)

    def make_bands(t, carry):
        enc = jnp.dot(enc_w[t], spread_mat, preferred_element_type=F32)
        dec = jnp.dot(dec_w[t], spread_mat, preferred_element_type=F32)
        enc_taps = [enc[c * channels : (c + 1) * channels] for c in range(3)]
        dec_taps = [
            [dec[(2 * c + s) * channels : (2 * c + s + 1) * channels] for c in range(3)]
            for s in range(2)
        ]
        for p in range(planes):
            rows = slice(p * channels, (p + 1) * channels)
            enc_band[t, rows] = band_block(enc_taps, p)
            for s in range(2):
                dec_band[t, s * width + p * channels : s * width + (p + 1) * channels] = band_block(
                    dec_taps[s], p
                )
        return carry

    lax.fori_loop(0, 9, make_bands, 0, unroll=9)

    wide[...] = jnp.zeros_like(wide)
    pre[...] = jnp.zeros_like(pre)
    acc_dec[...] = jnp.zeros_like(acc_dec)
    acc_cat[...] = jnp.zeros_like(acc_cat)
    g_dec[...] = jnp.zeros_like(g_dec)
    g_enc[...] = jnp.zeros_like(g_enc)

    arrive(halo_in)
    fill(wide, 2, mid_in, lo_in, hi_in)
    for b in range(3):
        near_in[b, :, 0:cy] = wide[:, BASE - 1 + b : BASE - 1 + b + cy].astype(BF16)
        tail = jnp.concatenate(
            [
                wide[:, BASE + cy - 1 + b : BASE + cy + 7 + b],
                wide[:, BASE - 9 + b : BASE - 1 + b],
            ],
            axis=1,
        )
        near_in[b, :, cy : cy + 16] = tail.astype(BF16)

    def enc_step(t, carry):
        a, b = t // 3, t % 3
        piece = near_in[b, pl.ds(a, cx + 2)].reshape((cx + 2) * (cy + 16), width)
        pre[...] += jnp.dot(piece, enc_band[t], preferred_element_type=F32)
        return carry

    lax.fori_loop(0, 9, enc_step, 0, unroll=9)

    value = pre[...].reshape(cx + 2, cy + 16, width)
    skip = (value * sigmoid(value)).astype(BF16).astype(F32)
    ext[:, BASE : BASE + cy] = skip[:, 0:cy]
    ext[:, BASE + cy : BASE + cy + 8] = skip[:, cy : cy + 8]
    ext[:, BASE - 8 : BASE] = skip[:, cy + 8 : cy + 16]
    spread(ext, near_sk)

    arrive(halo_co)
    fill(ext, 1, mid_co, lo_co, hi_co)
    spread(ext, near_co)

    def tap(near, t):
        a, b = t // 3, t % 3
        return near[b, pl.ds(a, cx)].reshape(cells, width)

    def tap_back(near, t):
        a, b = t // 3, t % 3
        return near[2 - b, pl.ds(2 - a, cx)].reshape(cells, width)

    def dec_step(t, carry):
        acc_dec[...] += jnp.dot(
            tap(near_co, t), dec_band[t, 0:width], preferred_element_type=F32
        ) + jnp.dot(tap(near_sk, t), dec_band[t, width : 2 * width], preferred_element_type=F32)
        return carry

    lax.fori_loop(0, 9, dec_step, 0, unroll=9)

    dec_own = (cotangent[...].astype(F32).reshape(cells, width) * slope(acc_dec[...])).astype(BF16)
    dec_cells = dec_own.reshape(cx, cy, width)
    mid_de[1 : 1 + cx] = dec_cells
    stage(dec_cells, 1, slo_de, shi_de)
    halo_de = halo(2, 1, mid_de, lo_de, hi_de, slo_de, shi_de)
    start(halo_de)

    group_of = lax.broadcasted_iota(jnp.int32, (channels, 128), 1) // channels
    row_group = lax.broadcasted_iota(jnp.int32, (8, 128), 1) // channels

    def by_group(index, parts):
        out = parts[-1]
        for g in range(len(parts) - 2, -1, -1):
            out = jnp.where(index == g, parts[g], out)
        return out

    def fold(product, c):
        parts = []
        for g in range(groups):
            total = None
            for z in range(g, planes, groups):
                p = z + c - 1
                if 0 <= p < planes:
                    lane = (z // groups) * 128
                    term = product[p * channels : (p + 1) * channels, lane : lane + 128]
                    total = term if total is None else total + term
            parts.append(total)
        both = by_group(group_of, parts)
        step = 64
        while step >= channels:
            both = both + pltpu.roll(both, step, 1)
            step //= 2
        return by_group(row_group, [both[8 * g : 8 * g + 8] for g in range(groups)])

    def contract(piece, delta):
        return lax.dot_general(piece, delta, (((0,), (0,)), ((), ())), preferred_element_type=F32)

    def dec_taps_step(t, carry):
        delta = mid_de[1 : 1 + cx].reshape(cells, width)
        for s, near in enumerate((near_co, near_sk)):
            product = contract(tap(near, t), delta)
            for c in range(3):
                g_dec[(t * 3 + c) * 2 + s] = fold(product, c)
        return carry

    lax.fori_loop(0, 9, dec_taps_step, 0, unroll=9)

    class Reduce:
        def __init__(self, which, g, r1, h, r2, f):
            self.g, self.r1, self.h, self.r2, self.f = g, r1, h, r2, f
            self.p1 = h.shape[0]
            self.p2 = r2.shape[1]
            mine = jy * self.p1 + ix * self.p2
            self.mine = mine
            self.y_scatter = []
            self.y_gather = []
            for k in range(1, ny):
                there = lax.rem(jy + k, ny)
                for phase, src, dst in (
                    (0, g.at[pl.ds(there * self.p1, self.p1)], r1.at[k - 1]),
                    (1, f.at[pl.ds(jy * self.p1, self.p1)], f.at[pl.ds(jy * self.p1, self.p1)]),
                ):
                    (self.y_scatter, self.y_gather)[phase].append(
                        pltpu.make_async_remote_copy(
                            src_ref=src,
                            dst_ref=dst,
                            send_sem=y_sems.at[which, phase, 0, k - 1],
                            recv_sem=y_sems.at[which, phase, 1, k - 1],
                            device_id=(ix, there),
                            device_id_type=MESH,
                        )
                    )
            self.x_scatter = []
            self.x_gather = []
            for k in range(1, nx):
                there = lax.rem(ix + k, nx)
                for phase, src, dst in (
                    (0, h.at[pl.ds(there * self.p2, self.p2)], r2.at[k - 1]),
                    (1, f.at[pl.ds(mine, self.p2)], f.at[pl.ds(mine, self.p2)]),
                ):
                    (self.x_scatter, self.x_gather)[phase].append(
                        pltpu.make_async_remote_copy(
                            src_ref=src,
                            dst_ref=dst,
                            send_sem=x_sems.at[which, phase, 0, k - 1],
                            recv_sem=x_sems.at[which, phase, 1, k - 1],
                            device_id=(there, jy),
                            device_id_type=MESH,
                        )
                    )

        def step1(self):
            start(self.y_scatter)

        def step2(self):
            arrive(self.y_scatter)
            total = self.g[pl.ds(jy * self.p1, self.p1)]
            for k in range(ny - 1):
                total = total + self.r1[k]
            self.h[...] = total
            start(self.x_scatter)

        def step3(self):
            arrive(self.x_scatter)
            total = self.h[pl.ds(ix * self.p2, self.p2)]
            for k in range(nx - 1):
                total = total + self.r2[k]
            self.f[pl.ds(self.mine, self.p2)] = total * scale
            start(self.x_gather)

        def step4(self):
            arrive(self.x_gather)
            start(self.y_gather)

        def step5(self):
            arrive(self.y_gather)

        def drain(self):
            for copy in self.y_scatter + self.x_scatter + self.x_gather + self.y_gather:
                copy.wait_send()

    dec_sum = Reduce(0, g_dec, r1_dec, h_dec, r2_dec, f_dec)
    enc_sum = Reduce(1, g_enc, r1_enc, h_enc, r2_enc, f_enc)
    dec_sum.step1()

    arrive(halo_de)
    fill(ext, 1, mid_de, lo_de, hi_de)
    spread(ext, near_de)

    def cat_step(t, carry):
        acc_cat[...] += lax.dot_general(
            tap_back(near_de, t), dec_band[t], (((1,), (1,)), ((), ())), preferred_element_type=F32
        )
        return carry

    lax.fori_loop(0, 9, cat_step, 0, unroll=9)
    coarse_grad[...] = acc_cat[:, 0:width].astype(BF16).reshape(cx, cy, width)
    pre_own = pre[...].reshape(cx + 2, cy + 16, width)[1 : 1 + cx, 0:cy].reshape(cells, width)
    enc_own = (acc_cat[:, width : 2 * width] * slope(pre_own)).astype(BF16)
    enc_cells = enc_own.reshape(cx, cy, width)
    mid_en[1 : 1 + cx] = enc_cells
    stage(enc_cells, 1, slo_en, shi_en)
    halo_en = halo(3, 1, mid_en, lo_en, hi_en, slo_en, shi_en)
    start(halo_en)
    dec_sum.step2()

    def enc_taps_step(t, carry):
        a, b = t // 3, t % 3
        delta = mid_en[1 : 1 + cx].reshape(cells, width)
        piece = near_in[b, pl.ds(a + 1, cx), 0:cy].reshape(cells, width)
        product = contract(piece, delta)
        for c in range(3):
            g_enc[t * 3 + c] = fold(product, c)
        return carry

    lax.fori_loop(0, 9, enc_taps_step, 0, unroll=9)
    enc_sum.step1()
    dec_sum.step3()

    arrive(halo_en)
    fill(ext, 1, mid_en, lo_en, hi_en)
    spread(ext, near_en)
    enc_sum.step2()
    acc_dec[...] = jnp.zeros_like(acc_dec)

    def back_step(t, carry):
        acc_dec[...] += lax.dot_general(
            tap_back(near_en, t), enc_band[t], (((1,), (1,)), ((), ())), preferred_element_type=F32
        )
        return carry

    lax.fori_loop(0, 9, back_step, 0, unroll=9)
    inputs_grad[...] = acc_dec[...].astype(BF16).reshape(cx, cy, width)

    enc_sum.step3()
    dec_sum.step4()
    enc_sum.step4()
    dec_sum.step5()

    def unpack_dec(t, carry):
        tile = f_dec[t]
        for g in range(groups):
            dec_out[t, g] = tile[:, g * channels : (g + 1) * channels]
        return carry

    lax.fori_loop(0, dec_out.shape[0], unpack_dec, 0, unroll=True)
    enc_sum.step5()

    def unpack_enc(t, carry):
        tile = f_enc[t]
        for g in range(groups):
            enc_out[t, g] = tile[:, g * channels : (g + 1) * channels]
        return carry

    lax.fori_loop(0, enc_out.shape[0], unpack_enc, 0, unroll=True)

    for copies in (halo_in, halo_co, halo_de, halo_en):
        for copy in copies:
            copy.wait_send()
    dec_sum.drain()
    enc_sum.drain()


def body(nx, ny, inputs, coarse, cotangent, enc_weight, dec_weight):
    cx, cy, width = inputs.shape
    channels = enc_weight.shape[3]
    planes = width // channels
    groups = 128 // channels
    rows = channels // groups
    cells = cx * cy
    scale = 1.0 / math.sqrt(cx * nx * cy * ny * planes)

    def halo_buffers(w):
        return [
            pltpu.VMEM((cx + 2 * w, cy, width), BF16),
            pltpu.VMEM((cx + 2 * w, w, width), F32),
            pltpu.VMEM((cx + 2 * w, w, width), F32),
            pltpu.VMEM((cx, w, width), F32),
            pltpu.VMEM((cx, w, width), F32),
        ]

    def sum_buffers(tiles):
        p2 = -(-tiles // (nx * ny))
        p1 = p2 * nx
        return [
            pltpu.VMEM((p1 * ny, 8, 128), F32),
            pltpu.VMEM((ny - 1, p1, 8, 128), F32),
            pltpu.VMEM((p1, 8, 128), F32),
            pltpu.VMEM((nx - 1, p2, 8, 128), F32),
            pltpu.VMEM((p1 * ny, 8, 128), F32),
        ]

    near = pltpu.VMEM((3, cx + 2, cy, width), BF16)
    vmem = pl.BlockSpec(memory_space=pltpu.VMEM)
    inputs_grad, coarse_grad, enc_total, dec_total = pl.pallas_call(
        functools.partial(kernel, nx, ny, scale),
        out_shape=(
            jax.ShapeDtypeStruct((cx, cy, width), BF16),
            jax.ShapeDtypeStruct((cx, cy, width), BF16),
            jax.ShapeDtypeStruct((27, groups, rows, channels), F32),
            jax.ShapeDtypeStruct((54, groups, rows, channels), F32),
        ),
        in_specs=[vmem] * 5,
        out_specs=(vmem,) * 4,
        scratch_shapes=[
            pltpu.VMEM((9, width, width), BF16),
            pltpu.VMEM((9, 2 * width, width), BF16),
            *halo_buffers(2),
            *halo_buffers(1),
            *halo_buffers(1),
            *halo_buffers(1),
            pltpu.VMEM((cx + 4, cy + 32, width), F32),
            pltpu.VMEM((cx + 2, cy + 32, width), F32),
            pltpu.VMEM((3, cx + 4, cy + 16, width), BF16),
            near,
            near,
            near,
            near,
            pltpu.VMEM(((cx + 2) * (cy + 16), width), F32),
            pltpu.VMEM((cells, width), F32),
            pltpu.VMEM((cells, 2 * width), F32),
            *sum_buffers(54),
            *sum_buffers(27),
            pltpu.SemaphoreType.DMA((4, 8)),
            pltpu.SemaphoreType.DMA((4, 8)),
            pltpu.SemaphoreType.DMA((2, 2, 2, ny - 1)),
            pltpu.SemaphoreType.DMA((2, 2, 2, nx - 1)),
        ],
        compiler_params=pltpu.CompilerParams(
            collective_id=0, has_side_effects=True, vmem_limit_bytes=48 << 20
        ),
    )(
        inputs,
        coarse,
        cotangent,
        enc_weight.reshape(9, 3 * channels, channels),
        dec_weight.reshape(9, 6 * channels, channels),
    )
    return (
        inputs_grad,
        coarse_grad,
        enc_total.reshape(3, 3, 3, channels, channels),
        dec_total.reshape(3, 3, 3, 2 * channels, channels),
    )


def solution(mesh):
    in_specs = (P("gx", "gy", None), P("gx", "gy", None), P("gx", "gy", None), P(), P())
    out_specs = (P("gx", "gy", None), P("gx", "gy", None), P(), P())
    return jax.shard_map(
        functools.partial(body, mesh.shape["gx"], mesh.shape["gy"]),
        mesh=mesh,
        in_specs=in_specs,
        out_specs=out_specs,
        check_vma=False,
    )
```

```python
import functools
import math

import jax
import jax.numpy as jnp
from jax import lax
from jax.experimental import pallas as pl
from jax.experimental.pallas import tpu as pltpu
from jax.sharding import PartitionSpec as P

MESH = pl.DeviceIdType.MESH
F32 = jnp.float32
BF16 = jnp.bfloat16
BASE = 16
DIRECTIONS = [(dx, dy) for dx in (-1, 0, 1) for dy in (-1, 0, 1) if (dx, dy) != (0, 0)]


def sigmoid(value):
    return 1.0 / (1.0 + jnp.exp(-value))


def slope(value):
    sig = sigmoid(value)
    return sig * (1.0 + value * (1.0 - sig))


def kernel(
    nx, ny, scale,
    inputs, coarse, cotangent, enc_w, dec_w,
    inputs_grad, coarse_grad, enc_out, dec_out,
    enc_band, dec_band,
    mid_in, lo_in, hi_in, slo_in, shi_in,
    mid_co, lo_co, hi_co, slo_co, shi_co,
    mid_de, lo_de, hi_de, slo_de, shi_de,
    mid_en, lo_en, hi_en, slo_en, shi_en,
    wide, ext, near_in, near_co, near_sk, near_de, near_en,
    pre, acc_dec, acc_cat,
    g_dec, r1_dec, h_dec, r2_dec, f_dec,
    g_enc, r1_enc, h_enc, r2_enc, f_enc,
    halo_send, halo_recv, y_sems, x_sems,
):
    ix = lax.axis_index("gx")
    jy = lax.axis_index("gy")
    cx, cy, width = inputs.shape
    cells = cx * cy
    channels = enc_w.shape[2]
    planes = width // channels
    groups = 128 // channels

    def peer(dx, dy):
        return (lax.rem(ix + dx + nx, nx), lax.rem(jy + dy + ny, ny))

    partners = {(dx % nx, dy % ny) for dx, dy in DIRECTIONS}
    partners |= {(k, 0) for k in range(1, nx)} | {(0, k) for k in range(1, ny)}
    barrier = pltpu.get_barrier_semaphore()
    for dx, dy in sorted(partners):
        pl.semaphore_signal(barrier, inc=1, device_id=peer(dx, dy), device_id_type=MESH)

    def stage(value, w, slo, shi):
        slo[...] = value[:, 0:w].astype(F32)
        shi[...] = value[:, cy - w : cy].astype(F32)

    def halo(which, w, mid, lo, hi, slo, shi):
        src_x = {-1: (0, w), 0: (0, cx), 1: (cx - w, w)}
        dst_x = {-1: (cx + w, w), 0: (w, cx), 1: (0, w)}
        copies = []
        for d, (dx, dy) in enumerate(DIRECTIONS):
            start, size = src_x[dx]
            if dy == 0:
                source = mid.at[pl.ds(w + start, size)]
            else:
                source = (slo if dy < 0 else shi).at[pl.ds(start, size)]
            target = {0: mid, -1: hi, 1: lo}[dy].at[pl.ds(dst_x[dx][0], size)]
            copies.append(
                pltpu.make_async_remote_copy(
                    src_ref=source,
                    dst_ref=target,
                    send_sem=halo_send.at[which, d],
                    recv_sem=halo_recv.at[which, d],
                    device_id=peer(dx, dy),
                    device_id_type=MESH,
                )
            )
        return copies

    def start(copies):
        for copy in copies:
            copy.start()

    def arrive(copies):
        for copy in copies:
            copy.wait_recv()

    def fill(target, w, mid, lo, hi):
        target[:, BASE : BASE + cy] = mid[...].astype(F32)
        target[:, BASE - w : BASE] = lo[...]
        target[:, BASE + cy : BASE + cy + w] = hi[...]

    def spread(source, near):
        for b in range(3):
            near[b] = source[:, BASE - 1 + b : BASE - 1 + b + cy].astype(BF16)

    own_in = inputs[...]
    own_co = coarse[...]
    mid_in[2 : 2 + cx] = own_in
    mid_co[1 : 1 + cx] = own_co
    stage(own_in, 2, slo_in, shi_in)
    stage(own_co, 1, slo_co, shi_co)
    pl.semaphore_wait(barrier, len(partners))
    halo_in = halo(0, 2, mid_in, lo_in, hi_in, slo_in, shi_in)
    halo_co = halo(1, 1, mid_co, lo_co, hi_co, slo_co, shi_co)
    start(halo_in)
    start(halo_co)

    spread_mat = (
        lax.broadcasted_iota(jnp.int32, (channels, width), 1) % channels
        == lax.broadcasted_iota(jnp.int32, (channels, width), 0)
    ).astype(F32).astype(BF16)
    plane_of = lax.broadcasted_iota(jnp.int32, (channels, width), 1) // channels

    def band_block(taps, p):
        block = jnp.where(plane_of == p - 1, taps[2], 0.0)
        block = jnp.where(plane_of == p, taps[1], block)
        return jnp.where(plane_of == p + 1, taps[0], block).astype(BF16)

    def make_bands(t, carry):
        enc = jnp.dot(enc_w[t], spread_mat, preferred_element_type=F32)
        dec = jnp.dot(dec_w[t], spread_mat, preferred_element_type=F32)
        enc_taps = [enc[c * channels : (c + 1) * channels] for c in range(3)]
        dec_taps = [
            [dec[(2 * c + s) * channels : (2 * c + s + 1) * channels] for c in range(3)]
            for s in range(2)
        ]
        for p in range(planes):
            rows = slice(p * channels, (p + 1) * channels)
            enc_band[t, rows] = band_block(enc_taps, p)
            for s in range(2):
                dec_band[t, s * width + p * channels : s * width + (p + 1) * channels] = band_block(
                    dec_taps[s], p
                )
        return carry

    lax.fori_loop(0, 9, make_bands, 0, unroll=9)

    wide[...] = jnp.zeros_like(wide)
    pre[...] = jnp.zeros_like(pre)
    acc_dec[...] = jnp.zeros_like(acc_dec)
    acc_cat[...] = jnp.zeros_like(acc_cat)
    g_dec[...] = jnp.zeros_like(g_dec)
    g_enc[...] = jnp.zeros_like(g_enc)

    arrive(halo_in)
    fill(wide, 2, mid_in, lo_in, hi_in)
    for b in range(3):
        near_in[b, :, 0:cy] = wide[:, BASE - 1 + b : BASE - 1 + b + cy].astype(BF16)
        tail = jnp.concatenate(
            [
                wide[:, BASE + cy - 1 + b : BASE + cy + 7 + b],
                wide[:, BASE - 9 + b : BASE - 1 + b],
            ],
            axis=1,
        )
        near_in[b, :, cy : cy + 16] = tail.astype(BF16)

    def enc_step(t, carry):
        a, b = t // 3, t % 3
        piece = near_in[b, pl.ds(a, cx + 2)].reshape((cx + 2) * (cy + 16), width)
        pre[...] += jnp.dot(piece, enc_band[t], preferred_element_type=F32)
        return carry

    lax.fori_loop(0, 9, enc_step, 0, unroll=9)

    value = pre[...].reshape(cx + 2, cy + 16, width)
    skip = (value * sigmoid(value)).astype(BF16).astype(F32)
    ext[:, BASE : BASE + cy] = skip[:, 0:cy]
    ext[:, BASE + cy : BASE + cy + 8] = skip[:, cy : cy + 8]
    ext[:, BASE - 8 : BASE] = skip[:, cy + 8 : cy + 16]
    spread(ext, near_sk)

    arrive(halo_co)
    fill(ext, 1, mid_co, lo_co, hi_co)
    spread(ext, near_co)

    def tap(near, t):
        a, b = t // 3, t % 3
        return near[b, pl.ds(a, cx)].reshape(cells, width)

    def tap_back(near, t):
        a, b = t // 3, t % 3
        return near[2 - b, pl.ds(2 - a, cx)].reshape(cells, width)

    def dec_step(t, carry):
        acc_dec[...] += jnp.dot(
            tap(near_co, t), dec_band[t, 0:width], preferred_element_type=F32
        ) + jnp.dot(tap(near_sk, t), dec_band[t, width : 2 * width], preferred_element_type=F32)
        return carry

    lax.fori_loop(0, 9, dec_step, 0, unroll=9)

    dec_own = (cotangent[...].astype(F32).reshape(cells, width) * slope(acc_dec[...])).astype(BF16)
    dec_cells = dec_own.reshape(cx, cy, width)
    mid_de[1 : 1 + cx] = dec_cells
    stage(dec_cells, 1, slo_de, shi_de)
    halo_de = halo(2, 1, mid_de, lo_de, hi_de, slo_de, shi_de)
    start(halo_de)

    group_of = lax.broadcasted_iota(jnp.int32, (channels, 128), 1) // channels
    row_group = lax.broadcasted_iota(jnp.int32, (8, 128), 1) // channels

    def by_group(index, parts):
        out = parts[-1]
        for g in range(len(parts) - 2, -1, -1):
            out = jnp.where(index == g, parts[g], out)
        return out

    def fold(product, c):
        parts = []
        for g in range(groups):
            total = None
            for z in range(g, planes, groups):
                p = z + c - 1
                if 0 <= p < planes:
                    lane = (z // groups) * 128
                    term = product[p * channels : (p + 1) * channels, lane : lane + 128]
                    total = term if total is None else total + term
            parts.append(total)
        both = by_group(group_of, parts)
        step = 64
        while step >= channels:
            both = both + pltpu.roll(both, step, 1)
            step //= 2
        return by_group(row_group, [both[8 * g : 8 * g + 8] for g in range(groups)])

    def contract(piece, delta):
        return lax.dot_general(piece, delta, (((0,), (0,)), ((), ())), preferred_element_type=F32)

    def dec_taps_step(t, carry):
        delta = mid_de[1 : 1 + cx].reshape(cells, width)
        for s, near in enumerate((near_co, near_sk)):
            product = contract(tap(near, t), delta)
            for c in range(3):
                g_dec[(t * 3 + c) * 2 + s] = fold(product, c)
        return carry

    lax.fori_loop(0, 9, dec_taps_step, 0, unroll=9)

    class Reduce:
        def __init__(self, which, g, r1, h, r2, f):
            self.g, self.r1, self.h, self.r2, self.f = g, r1, h, r2, f
            self.p1 = h.shape[0]
            self.p2 = r2.shape[1]
            mine = jy * self.p1 + ix * self.p2
            self.mine = mine
            self.y_scatter = []
            self.y_gather = []
            for k in range(1, ny):
                there = lax.rem(jy + k, ny)
                for phase, src, dst in (
                    (0, g.at[pl.ds(there * self.p1, self.p1)], r1.at[k - 1]),
                    (1, f.at[pl.ds(jy * self.p1, self.p1)], f.at[pl.ds(jy * self.p1, self.p1)]),
                ):
                    (self.y_scatter, self.y_gather)[phase].append(
                        pltpu.make_async_remote_copy(
                            src_ref=src,
                            dst_ref=dst,
                            send_sem=y_sems.at[which, phase, 0, k - 1],
                            recv_sem=y_sems.at[which, phase, 1, k - 1],
                            device_id=(ix, there),
                            device_id_type=MESH,
                        )
                    )
            self.x_scatter = []
            self.x_gather = []
            for k in range(1, nx):
                there = lax.rem(ix + k, nx)
                for phase, src, dst in (
                    (0, h.at[pl.ds(there * self.p2, self.p2)], r2.at[k - 1]),
                    (1, f.at[pl.ds(mine, self.p2)], f.at[pl.ds(mine, self.p2)]),
                ):
                    (self.x_scatter, self.x_gather)[phase].append(
                        pltpu.make_async_remote_copy(
                            src_ref=src,
                            dst_ref=dst,
                            send_sem=x_sems.at[which, phase, 0, k - 1],
                            recv_sem=x_sems.at[which, phase, 1, k - 1],
                            device_id=(there, jy),
                            device_id_type=MESH,
                        )
                    )

        def step1(self):
            start(self.y_scatter)

        def step2(self):
            arrive(self.y_scatter)
            total = self.g[pl.ds(jy * self.p1, self.p1)]
            for k in range(ny - 1):
                total = total + self.r1[k]
            self.h[...] = total
            start(self.x_scatter)

        def step3(self):
            arrive(self.x_scatter)
            total = self.h[pl.ds(ix * self.p2, self.p2)]
            for k in range(nx - 1):
                total = total + self.r2[k]
            self.f[pl.ds(self.mine, self.p2)] = total * scale
            start(self.x_gather)

        def step4(self):
            arrive(self.x_gather)
            start(self.y_gather)

        def step5(self):
            arrive(self.y_gather)

        def drain(self):
            for copy in self.y_scatter + self.x_scatter + self.x_gather + self.y_gather:
                copy.wait_send()

    dec_sum = Reduce(0, g_dec, r1_dec, h_dec, r2_dec, f_dec)
    enc_sum = Reduce(1, g_enc, r1_enc, h_enc, r2_enc, f_enc)
    dec_sum.step1()

    arrive(halo_de)
    fill(ext, 1, mid_de, lo_de, hi_de)
    spread(ext, near_de)

    def cat_step(t, carry):
        acc_cat[...] += lax.dot_general(
            tap_back(near_de, t), dec_band[t], (((1,), (1,)), ((), ())), preferred_element_type=F32
        )
        return carry

    lax.fori_loop(0, 9, cat_step, 0, unroll=9)
    coarse_grad[...] = acc_cat[:, 0:width].astype(BF16).reshape(cx, cy, width)
    pre_own = pre[...].reshape(cx + 2, cy + 16, width)[1 : 1 + cx, 0:cy].reshape(cells, width)
    enc_own = (acc_cat[:, width : 2 * width] * slope(pre_own)).astype(BF16)
    enc_cells = enc_own.reshape(cx, cy, width)
    mid_en[1 : 1 + cx] = enc_cells
    stage(enc_cells, 1, slo_en, shi_en)
    halo_en = halo(3, 1, mid_en, lo_en, hi_en, slo_en, shi_en)
    start(halo_en)
    dec_sum.step2()

    def enc_taps_step(t, carry):
        a, b = t // 3, t % 3
        delta = mid_en[1 : 1 + cx].reshape(cells, width)
        piece = near_in[b, pl.ds(a + 1, cx), 0:cy].reshape(cells, width)
        product = contract(piece, delta)
        for c in range(3):
            g_enc[t * 3 + c] = fold(product, c)
        return carry

    lax.fori_loop(0, 9, enc_taps_step, 0, unroll=9)
    enc_sum.step1()
    dec_sum.step3()

    arrive(halo_en)
    fill(ext, 1, mid_en, lo_en, hi_en)
    spread(ext, near_en)
    enc_sum.step2()
    acc_dec[...] = jnp.zeros_like(acc_dec)

    def back_step(t, carry):
        acc_dec[...] += lax.dot_general(
            tap_back(near_en, t), enc_band[t], (((1,), (1,)), ((), ())), preferred_element_type=F32
        )
        return carry

    lax.fori_loop(0, 9, back_step, 0, unroll=9)
    inputs_grad[...] = acc_dec[...].astype(BF16).reshape(cx, cy, width)

    dec_sum.step4()
    enc_sum.step3()
    dec_sum.step5()

    def unpack_dec(t, carry):
        tile = f_dec[t]
        for g in range(groups):
            dec_out[t, g] = tile[:, g * channels : (g + 1) * channels]
        return carry

    lax.fori_loop(0, dec_out.shape[0], unpack_dec, 0, unroll=True)
    enc_sum.step4()
    enc_sum.step5()

    def unpack_enc(t, carry):
        tile = f_enc[t]
        for g in range(groups):
            enc_out[t, g] = tile[:, g * channels : (g + 1) * channels]
        return carry

    lax.fori_loop(0, enc_out.shape[0], unpack_enc, 0, unroll=True)

    for copies in (halo_in, halo_co, halo_de, halo_en):
        for copy in copies:
            copy.wait_send()
    dec_sum.drain()
    enc_sum.drain()


def body(nx, ny, inputs, coarse, cotangent, enc_weight, dec_weight):
    cx, cy, width = inputs.shape
    channels = enc_weight.shape[3]
    planes = width // channels
    groups = 128 // channels
    rows = channels // groups
    cells = cx * cy
    scale = 1.0 / math.sqrt(cx * nx * cy * ny * planes)

    def halo_buffers(w):
        return [
            pltpu.VMEM((cx + 2 * w, cy, width), BF16),
            pltpu.VMEM((cx + 2 * w, w, width), F32),
            pltpu.VMEM((cx + 2 * w, w, width), F32),
            pltpu.VMEM((cx, w, width), F32),
            pltpu.VMEM((cx, w, width), F32),
        ]

    def sum_buffers(tiles):
        p2 = -(-tiles // (nx * ny))
        p1 = p2 * nx
        return [
            pltpu.VMEM((p1 * ny, 8, 128), F32),
            pltpu.VMEM((ny - 1, p1, 8, 128), F32),
            pltpu.VMEM((p1, 8, 128), F32),
            pltpu.VMEM((nx - 1, p2, 8, 128), F32),
            pltpu.VMEM((p1 * ny, 8, 128), F32),
        ]

    near = pltpu.VMEM((3, cx + 2, cy, width), BF16)
    vmem = pl.BlockSpec(memory_space=pltpu.VMEM)
    inputs_grad, coarse_grad, enc_total, dec_total = pl.pallas_call(
        functools.partial(kernel, nx, ny, scale),
        out_shape=(
            jax.ShapeDtypeStruct((cx, cy, width), BF16),
            jax.ShapeDtypeStruct((cx, cy, width), BF16),
            jax.ShapeDtypeStruct((27, groups, rows, channels), F32),
            jax.ShapeDtypeStruct((54, groups, rows, channels), F32),
        ),
        in_specs=[vmem] * 5,
        out_specs=(vmem,) * 4,
        scratch_shapes=[
            pltpu.VMEM((9, width, width), BF16),
            pltpu.VMEM((9, 2 * width, width), BF16),
            *halo_buffers(2),
            *halo_buffers(1),
            *halo_buffers(1),
            *halo_buffers(1),
            pltpu.VMEM((cx + 4, cy + 32, width), F32),
            pltpu.VMEM((cx + 2, cy + 32, width), F32),
            pltpu.VMEM((3, cx + 4, cy + 16, width), BF16),
            near,
            near,
            near,
            near,
            pltpu.VMEM(((cx + 2) * (cy + 16), width), F32),
            pltpu.VMEM((cells, width), F32),
            pltpu.VMEM((cells, 2 * width), F32),
            *sum_buffers(54),
            *sum_buffers(27),
            pltpu.SemaphoreType.DMA((4, 8)),
            pltpu.SemaphoreType.DMA((4, 8)),
            pltpu.SemaphoreType.DMA((2, 2, 2, ny - 1)),
            pltpu.SemaphoreType.DMA((2, 2, 2, nx - 1)),
        ],
        compiler_params=pltpu.CompilerParams(
            collective_id=0, has_side_effects=True, vmem_limit_bytes=48 << 20
        ),
    )(
        inputs,
        coarse,
        cotangent,
        enc_weight.reshape(9, 3 * channels, channels),
        dec_weight.reshape(9, 6 * channels, channels),
    )
    return (
        inputs_grad,
        coarse_grad,
        enc_total.reshape(3, 3, 3, channels, channels),
        dec_total.reshape(3, 3, 3, 2 * channels, channels),
    )


def solution(mesh):
    in_specs = (P("gx", "gy", None), P("gx", "gy", None), P("gx", "gy", None), P(), P())
    out_specs = (P("gx", "gy", None), P("gx", "gy", None), P(), P())
    return jax.shard_map(
        functools.partial(body, mesh.shape["gx"], mesh.shape["gy"]),
        mesh=mesh,
        in_specs=in_specs,
        out_specs=out_specs,
        check_vma=False,
    )
```
